32 devices in a mesh: stream: 4 (over z), cross: 4 (over y, x), pair: 2 (over core).
Axes of the slice: x: 2, y: 2, z: 4, core: 2. Of those that a mesh axis runs over, the one named last changes fastest.
Arguments:
- krylov_basis: float32 [4, 4, 4, 64, 320], P(None, None, 'stream', ('cross', 'pair')), may hold values from -6 to 6
- inverse_blocks: bfloat16 [4, 64, 320, 320], P('stream', ('cross', 'pair'))
- inflow_lift: bfloat16 [4, 64, 320, 80], P('stream', ('cross', 'pair')), may hold values from -0.625 to 0.625
- outflow_trace: bfloat16 [4, 64, 80, 320], P('stream', ('cross', 'pair')), may hold values from -0.3125 to 0.3125
- cross_lift: bfloat16 [4, 64, 320, 80], P('stream', ('cross', 'pair')), may hold values from -0.625 to 0.625
- cross_trace: bfloat16 [4, 64, 80, 320], P('stream', ('cross', 'pair')), may hold values from -0.3125 to 0.3125
- upwind_element: int32 [4, 64], P('stream', ('cross', 'pair')), may hold values from 0 to 7
- cross_element: int32 [4, 64], P('stream', ('cross', 'pair')), may hold values from 0 to 63
Outputs:
- next_vector: float32 [4, 4, 64, 320], P(None, 'stream', ('cross', 'pair'))
- hessenberg: float32 [5, 4], replicated
The draws below stay inside these ranges and needn't reach their ends.
Inputs may be any that keep to these rules, and one draw needn't show every extreme that they name: upwind_element names one of the 8 elements held by the device one partition upstream at the same cross-stream place; at streamwise position 0 it is not read. cross_element names any element at the same streamwise position.
All inputs are finite; a program needn't handle non-finite values.
Results may differ from the reference program's by a relative error of at most 0.0003.
Values sent between devices are 32-bit elements; how exact they have to be, the bound alone decides.
A program may use at most 64 MiB of HBM per device.

```python
import jax
import jax.numpy as jnp
from jax import lax

E = 8
B = 320
R = 80
NV = 4
KB = 4
S = 4
G = 64


def draw_inverse_blocks(key, part):
    key_diag = jax.random.fold_in(key, 11)
    key_off = jax.random.fold_in(key, 23)
    diagonal = jnp.exp(jax.random.uniform(key_diag, (S, G, B), jnp.float32, jnp.log(0.5), jnp.log(2.0)))
    off_part = jax.random.normal(key_off, (S, G, B, B), jnp.float32) * (0.5 / jnp.sqrt(1.0 * B))
    blocks = diagonal[..., None] * jnp.eye(B, dtype=jnp.float32) + off_part
    return blocks.astype(jnp.bfloat16)


def plant(array, rng, low, largest):
    longest = array.shape.index(max(array.shape))
    spots = []
    for shift in (0, 1):
        where = [jax.random.randint(jax.random.fold_in(rng, axis), (), 0, length) for axis, length in enumerate(array.shape)]
        where[longest] = (where[longest] + shift) % array.shape[longest]
        spots.append(tuple(where))
    return array.at[spots[0]].set(low).at[spots[1]].set(largest)


def block_levels(own_key, extent, pieces, least, high):
    level = 1.0
    for position, parts in pieces:
        heights = jax.random.uniform(jax.random.fold_in(jax.random.fold_in(own_key, 6), position), (parts,), jnp.float32, least / len(pieces), high / len(pieces))
        level = level * jnp.repeat(jnp.exp(heights), extent[position] // parts).reshape((-1,) + (1,) * (len(extent) - 1 - position))
    return level


def scatter_about(own_key, extent, width, most, cuts=(), kind=jnp.bfloat16):
    entries = jax.random.normal(own_key, extent, jnp.float32) * width
    if len(cuts) > 0:
        entries = block_levels(own_key, extent, cuts, -0.22, 0.18) * entries
    return jnp.clip(entries, min=-most, max=most).astype(kind)


def setup_inputs(seed: int = 0) -> dict:
    arg_keys = jax.random.split(jax.random.key(seed), 9)
    return {
        "krylov_basis": scatter_about(arg_keys[0], (KB, NV, S, G, B), 1.0, 6.0, ((2, 4), (3, 8)), jnp.float32),
        "inverse_blocks": draw_inverse_blocks(jax.random.fold_in(arg_keys[8], 71), 0),
        "inflow_lift": scatter_about(arg_keys[2], (S, G, B, R), R ** -0.5, 0.625, ((0, 4), (1, 8))),
        "outflow_trace": scatter_about(arg_keys[3], (S, G, R, B), B ** -0.5, 0.3125, ((0, 4), (1, 8))),
        "cross_lift": scatter_about(arg_keys[4], (S, G, B, R), R ** -0.5, 0.625, ((0, 4), (1, 8))),
        "cross_trace": scatter_about(arg_keys[5], (S, G, R, B), B ** -0.5, 0.3125, ((0, 4), (1, 8))),
        "upwind_element": plant(jax.random.randint(arg_keys[6], (S, G), 0, E), jax.random.fold_in(arg_keys[6], 1), 0, E - 1).astype(jnp.int32),
        "cross_element": plant(jax.random.randint(arg_keys[7], (S, G), 0, G), jax.random.fold_in(arg_keys[7], 1), 0, G - 1).astype(jnp.int32),
    }


def take_faces(face_slice, index_row):
    return jnp.take(face_slice, index_row, axis=1)

def reference(krylov_basis, inverse_blocks, inflow_lift, outflow_trace, cross_lift, cross_trace, upwind_element, cross_element):
    highest = lax.Precision.HIGHEST
    current = krylov_basis[KB - 1]
    group_start = jnp.arange(G, dtype=jnp.int32) // E * E

    def advance(previous, sliced):
        inverse_slice, lift_slice, trace_slice, upwind_slice, vector_slice = sliced
        inflow = jnp.take(previous, group_start + upwind_slice, axis=1)
        right_side = vector_slice - jnp.einsum('gbr,ngr->ngb', lift_slice.astype(jnp.float32), inflow, precision=highest)
        relaxed = jnp.einsum('gbc,ngc->ngb', inverse_slice.astype(jnp.float32), right_side, precision=highest)
        outflow = jnp.einsum('grb,ngb->ngr', trace_slice.astype(jnp.float32), relaxed, precision=highest)
        return (outflow, relaxed)
    start_state = jnp.zeros((NV, G, R), jnp.float32)
    _, solved = lax.scan(advance, start_state, (inverse_blocks, inflow_lift, outflow_trace, upwind_element, jnp.moveaxis(current, 1, 0)))
    relaxed = jnp.moveaxis(solved, 0, 1)
    face_data = jnp.einsum('sgrb,nsgb->nsgr', cross_trace.astype(jnp.float32), relaxed, precision=highest)
    read_faces = jax.vmap(take_faces, in_axes=(1, 0), out_axes=1)(face_data, cross_element)
    image = current + jnp.einsum('sgbr,nsgr->nsgb', cross_lift.astype(jnp.float32), read_faces, precision=highest)
    total_dofs = float(S * G * B)
    coeffs = jnp.einsum('knsgb,nsgb->kn', krylov_basis, image, precision=highest) / total_dofs
    orthogonal = image - jnp.einsum('kn,knsgb->nsgb', coeffs, krylov_basis, precision=highest)
    new_norm = jnp.sqrt(lax.optimization_barrier(jnp.sum(orthogonal * orthogonal, axis=(1, 2, 3))) / total_dofs + 1e-06)
    next_vector = orthogonal / new_norm[:, None, None, None]
    return (next_vector, jnp.concatenate([coeffs, new_norm[None, :]], axis=0))
```

```python
import functools

import jax
import jax.numpy as jnp
from jax import lax
from jax.experimental import pallas as pl
from jax.experimental.pallas import tpu as pltpu
from jax.sharding import PartitionSpec as P

E = 8
B = 320
R = 80
NV = 4
KB = 4
MESH = pl.DeviceIdType.MESH
GRAM = [(k, l) for k in range(KB) for l in range(k, KB)]
STATS = KB + 1 + len(GRAM)
ROWS = 64
GROUP = 2


def split(x):
    hi = x.astype(jnp.bfloat16)
    return hi, (x - hi.astype(jnp.float32)).astype(jnp.bfloat16)


def dot(a, b):
    return jnp.dot(a, b, preferred_element_type=jnp.float32)


def dot_t(a, b):
    return lax.dot_general(a, b, (((1,), (1,)), ((), ())), preferred_element_type=jnp.float32)


def two_rows(x):
    hi = x.astype(jnp.bfloat16).astype(jnp.float32)
    return jnp.concatenate([hi, x - hi], axis=0).astype(jnp.bfloat16)


def fold(x):
    return x[:NV] + x[NV:]


def kernel(
    sizes,
    kry_hbm,
    inv_hbm,
    lift_hbm,
    otr_hbm,
    clift_hbm,
    ctr_hbm,
    up_ref,
    cr_ref,
    next_ref,
    hess_ref,
    kry,
    inv,
    lift,
    otr,
    clift,
    ctr,
    gain_o,
    gain_c,
    off_o,
    off_c,
    outbuf,
    inbuf,
    faces,
    dbuf,
    parts,
    stats,
    load_sem,
    hop_sem,
    face_sem,
    stat_sem,
):
    S, C, Q = sizes
    total = S * C * Q
    s = lax.axis_index("stream")
    c = lax.axis_index("cross")
    q = lax.axis_index("pair")
    place = c * Q + q
    me = s * (C * Q) + place

    kry_copy = pltpu.make_async_copy(kry_hbm, kry, load_sem.at[0])
    kry_copy.start()
    groups = []
    for g in range(E // GROUP):
        span = pl.ds(g * GROUP, GROUP)
        copies = [
            pltpu.make_async_copy(src.at[span], dst.at[span], load_sem.at[2 + 4 * g + i])
            for i, (src, dst) in enumerate(
                ((inv_hbm, inv), (otr_hbm, otr), (ctr_hbm, ctr), (lift_hbm, lift))
            )
        ]
        for copy in copies:
            copy.start()
        groups.append(copies)
    clift_copy = pltpu.make_async_copy(clift_hbm, clift, load_sem.at[1])
    clift_copy.start()

    barrier = pltpu.get_barrier_semaphore()

    def others():
        for ds in range(S):
            for dc in range(C):
                for dq in range(Q):
                    if ds or dc or dq:
                        yield (lax.rem(s + ds, S), lax.rem(c + dc, C), lax.rem(q + dq, Q))

    for peer in others():
        pl.semaphore_signal(barrier, inc=1, device_id=peer, device_id_type=MESH)

    kry_copy.wait()
    for g in range(E // GROUP):
        for copy in groups[g]:
            copy.wait()
        for e in range(g * GROUP, (g + 1) * GROUP):
            cur = kry[KB - 1, :, e, :]
            hi = cur.astype(jnp.bfloat16).astype(jnp.float32)
            rows = jnp.concatenate(
                [hi, cur - hi, jnp.zeros((8, B), jnp.float32)], axis=0
            ).astype(jnp.bfloat16)
            left = jnp.concatenate([lift[e], rows], axis=0)
            for trace, gain, off in ((otr, gain_o, off_o), (ctr, gain_c, off_c)):
                t_hi, t_lo = split(dot(trace[e], inv[e]))
                out = dot_t(left, t_hi) + dot_t(left, t_lo)
                g_hi, g_lo = split(out[:R])
                gain[e, 0] = g_hi
                gain[e, 1] = g_lo
                off[e] = out[R : R + NV] + out[R + NV : R + 2 * NV]

    def gram():
        for n in range(NV):
            vs = [kry[k, n] for k in range(KB)]
            for i, (k, l) in enumerate(GRAM):
                row = NV * (KB + 1 + i) + n
                parts[row : row + 1, :] = lanes(vs[k] * vs[l])
        parts[NV * STATS :, :] = jnp.zeros((ROWS - NV * STATS, 128), jnp.float32)

    def lanes(x):
        x = jnp.sum(x, axis=0, keepdims=True)
        tail = jnp.concatenate([x[:, 256:B], jnp.zeros((1, 384 - B), jnp.float32)], axis=1)
        return x[:, :128] + x[:, 128:256] + tail

    pl.semaphore_wait(barrier, total - 1)

    hop = pltpu.make_async_remote_copy(
        src_ref=outbuf,
        dst_ref=inbuf,
        send_sem=hop_sem.at[0],
        recv_sem=hop_sem.at[1],
        device_id=(lax.rem(s + 1, S), c, q),
        device_id_type=MESH,
    )

    def face_copy(dc, dq):
        span = pl.ds(place * E, E)
        return pltpu.make_async_remote_copy(
            src_ref=faces.at[span],
            dst_ref=faces.at[span],
            send_sem=face_sem.at[0],
            recv_sem=face_sem.at[1],
            device_id=(s, lax.rem(c + dc, C), lax.rem(q + dq, Q)),
            device_id_type=MESH,
        )

    def send_faces():
        for dc in range(C):
            for dq in range(Q):
                if dc or dq:
                    face_copy(dc, dq).start()

    @pl.when(s == 0)
    def _():
        for e in range(E):
            outbuf[e] = off_o[e]
        if S > 1:
            hop.start()
        for e in range(E):
            faces[place * E + e] = off_c[e]
        send_faces()
        gram()

    @pl.when(s > 0)
    def _():
        gram()
        hop.wait_recv()

        @pl.when(s < S - 1)
        def _():
            for e in range(E):
                x = two_rows(inbuf[up_ref[0, e]])
                outbuf[e] = off_o[e] - fold(dot(x, gain_o[e, 0]) + dot(x, gain_o[e, 1]))
            hop.start()

        for e in range(E):
            x = two_rows(inbuf[up_ref[0, e]])
            faces[place * E + e] = off_c[e] - fold(dot(x, gain_c[e, 0]) + dot(x, gain_c[e, 1]))
        send_faces()

    clift_copy.wait()
    peers = C * Q - 1
    face_all = pltpu.make_async_remote_copy(
        src_ref=faces.at[pl.ds(0, peers * E)],
        dst_ref=faces.at[pl.ds(0, peers * E)],
        send_sem=face_sem.at[0],
        recv_sem=face_sem.at[1],
        device_id=(s, c, lax.rem(q + 1, Q)),
        device_id_type=MESH,
    )
    face_all.wait_recv()

    for e in range(E):
        x = two_rows(faces[cr_ref[0, e]])
        dbuf[:, e, :] = fold(dot(x, clift[e]))

    for n in range(NV):
        d = dbuf[n]
        for k in range(KB):
            parts[NV * k + n : NV * k + n + 1, :] = lanes(kry[k, n] * d)
        parts[NV * KB + n : NV * KB + n + 1, :] = lanes(d * d)

    diag = lax.broadcasted_iota(jnp.int32, (ROWS, 128), 0) == lax.broadcasted_iota(
        jnp.int32, (ROWS, 128), 1
    )
    column = jnp.sum(parts[...], axis=1, keepdims=True)
    stats[me] = jnp.sum(jnp.where(diag, column, 0.0), axis=0, keepdims=True)

    def stat_copy(peer):
        return pltpu.make_async_remote_copy(
            src_ref=stats.at[me],
            dst_ref=stats.at[me],
            send_sem=stat_sem.at[0],
            recv_sem=stat_sem.at[1],
            device_id=peer,
            device_id_type=MESH,
        )

    for peer in others():
        stat_copy(peer).start()
    stat_all = pltpu.make_async_remote_copy(
        src_ref=stats.at[pl.ds(0, total - 1)],
        dst_ref=stats.at[pl.ds(0, total - 1)],
        send_sem=stat_sem.at[0],
        recv_sem=stat_sem.at[1],
        device_id=(s, c, lax.rem(q + 1, Q)),
        device_id_type=MESH,
    )
    stat_all.wait_recv()

    row = jnp.sum(stats[...], axis=0)
    sums = jnp.sum(jnp.where(diag, row, 0.0), axis=1, keepdims=True)
    at = lambda i: sums[NV * i : NV * (i + 1)]
    dofs = float(E * B * total)
    entry = {}
    for i, (k, l) in enumerate(GRAM):
        entry[k, l] = entry[l, k] = at(KB + 1 + i)
    coeffs = [(entry[k, KB - 1] + at(k)) / dofs for k in range(KB)]
    rest = [(1.0 if k == KB - 1 else 0.0) - coeffs[k] for k in range(KB)]
    squares = at(KB)
    for k in range(KB):
        inner = 2.0 * at(k)
        for l in range(KB):
            inner += rest[l] * entry[k, l]
        squares += rest[k] * inner
    norm = jnp.sqrt(jnp.maximum(squares, 0.0) / dofs + 1e-06)
    scale = 1.0 / norm
    weights = [r * scale for r in rest]
    for n in range(NV):
        out = dbuf[n] * scale[n : n + 1]
        for k in range(KB):
            out += kry[k, n] * weights[k][n : n + 1]
        next_ref[n] = out
    hess_ref[...] = jnp.concatenate(coeffs + [norm], axis=1)
    face_all.wait_send()
    stat_all.wait_send()

    @pl.when(s < S - 1)
    def _():
        hop.wait_send()


def local(
    sizes,
    krylov_basis,
    inverse_blocks,
    inflow_lift,
    outflow_trace,
    cross_lift,
    cross_trace,
    upwind_element,
    cross_element,
):
    S, C, Q = sizes
    hbm = pl.BlockSpec(memory_space=pl.ANY)
    smem = pl.BlockSpec(memory_space=pltpu.SMEM)
    vmem = pl.BlockSpec(memory_space=pltpu.VMEM)
    bf16, f32 = jnp.bfloat16, jnp.float32
    next_vector, hessenberg = pl.pallas_call(
        functools.partial(kernel, sizes),
        out_shape=(
            jax.ShapeDtypeStruct((NV, E, B), f32),
            jax.ShapeDtypeStruct((NV, KB + 1), f32),
        ),
        in_specs=[hbm] * 6 + [smem] * 2,
        out_specs=(vmem, vmem),
        scratch_shapes=[
            pltpu.VMEM((KB, NV, E, B), f32),
            pltpu.VMEM((E, B, B), bf16),
            pltpu.VMEM((E, R, B), bf16),
            pltpu.VMEM((E, R, B), bf16),
            pltpu.VMEM((E, R, B), bf16),
            pltpu.VMEM((E, R, B), bf16),
            pltpu.VMEM((E, 2, R, R), bf16),
            pltpu.VMEM((E, 2, R, R), bf16),
            pltpu.VMEM((E, NV, R), f32),
            pltpu.VMEM((E, NV, R), f32),
            pltpu.VMEM((E, NV, R), f32),
            pltpu.VMEM((E, NV, R), f32),
            pltpu.VMEM((C * Q * E, NV, R), f32),
            pltpu.VMEM((NV, E, B), f32),
            pltpu.VMEM((ROWS, 128), f32),
            pltpu.VMEM((S * C * Q, 1, 128), f32),
            pltpu.SemaphoreType.DMA((2 + 4 * (E // GROUP),)),
            pltpu.SemaphoreType.DMA((2,)),
            pltpu.SemaphoreType.DMA((2,)),
            pltpu.SemaphoreType.DMA((2,)),
        ],
        compiler_params=pltpu.CompilerParams(collective_id=0, has_side_effects=True),
    )(
        krylov_basis[:, :, 0],
        inverse_blocks[0],
        jnp.swapaxes(inflow_lift[0], 1, 2),
        outflow_trace[0],
        jnp.swapaxes(cross_lift[0], 1, 2),
        cross_trace[0],
        upwind_element,
        cross_element,
    )
    return next_vector[:, None], hessenberg.T


def solution(mesh):
    sizes = tuple(mesh.shape[a] for a in ("stream", "cross", "pair"))
    return jax.shard_map(
        functools.partial(local, sizes),
        mesh=mesh,
        in_specs=(
            P(None, None, "stream", ("cross", "pair"), None),
            P("stream", ("cross", "pair"), None, None),
            P("stream", ("cross", "pair"), None, None),
            P("stream", ("cross", "pair"), None, None),
            P("stream", ("cross", "pair"), None, None),
            P("stream", ("cross", "pair"), None, None),
            P("stream", ("cross", "pair")),
            P("stream", ("cross", "pair")),
        ),
        out_specs=(P(None, "stream", ("cross", "pair"), None), P()),
        check_vma=False,
    )
```

```python
import functools

import jax
import jax.numpy as jnp
from jax import lax
from jax.experimental import pallas as pl
from jax.experimental.pallas import tpu as pltpu
from jax.sharding import PartitionSpec as P

E = 8
B = 320
R = 80
NV = 4
KB = 4
MESH = pl.DeviceIdType.MESH
GRAM = [(k, l) for k in range(KB) for l in range(k, KB)]
STATS = KB + 1 + len(GRAM)
ROWS = 64
GROUP = 2


def split(x):
    hi = x.astype(jnp.bfloat16)
    return hi, (x - hi.astype(jnp.float32)).astype(jnp.bfloat16)


def dot(a, b):
    return jnp.dot(a, b, preferred_element_type=jnp.float32)


def dot_t(a, b):
    return lax.dot_general(a, b, (((1,), (1,)), ((), ())), preferred_element_type=jnp.float32)


def two_rows(x):
    hi = x.astype(jnp.bfloat16).astype(jnp.float32)
    return jnp.concatenate([hi, x - hi], axis=0).astype(jnp.bfloat16)


def fold(x):
    return x[:NV] + x[NV:]


def kernel(
    sizes,
    kry_hbm,
    inv_hbm,
    lift_hbm,
    otr_hbm,
    clift_hbm,
    ctr_hbm,
    up_ref,
    cr_ref,
    d_hbm,
    row_ref,
    kry,
    inv,
    lift,
    otr,
    clift,
    ctr,
    solved,
    gain_o,
    gain_c,
    off_o,
    off_c,
    outbuf,
    inbuf,
    faces,
    dbuf,
    parts,
    stats,
    load_sem,
    hop_sem,
    face_sem,
    stat_sem,
    out_sem,
    back_sem,
):
    S, C, Q = sizes
    total = S * C * Q
    s = lax.axis_index("stream")
    c = lax.axis_index("cross")
    q = lax.axis_index("pair")
    place = c * Q + q
    me = s * (C * Q) + place

    barrier = pltpu.get_barrier_semaphore()

    def others():
        for ds in range(S):
            for dc in range(C):
                for dq in range(Q):
                    if ds or dc or dq:
                        yield (lax.rem(s + ds, S), lax.rem(c + dc, C), lax.rem(q + dq, Q))

    for dc in range(C):
        for dq in range(Q):
            if dc or dq:
                pl.semaphore_signal(
                    barrier,
                    inc=1,
                    device_id=(s, lax.rem(c + dc, C), lax.rem(q + dq, Q)),
                    device_id_type=MESH,
                )
    for edge, step in ((S - 1, 1), (0, S - 1)):

        @pl.when(s != edge)
        def _():
            pl.semaphore_signal(
                barrier, inc=1, device_id=(lax.rem(s + step, S), c, q), device_id_type=MESH
            )

    kry_copy = pltpu.make_async_copy(kry_hbm, kry, load_sem.at[0])
    inv_copies = [
        pltpu.make_async_copy(
            inv_hbm.at[pl.ds(g * GROUP, GROUP)], inv.at[pl.ds(g * GROUP, GROUP)], load_sem.at[5 + g]
        )
        for g in range(E // GROUP)
    ]
    otr_copy = pltpu.make_async_copy(otr_hbm, otr, load_sem.at[1])
    lift_copy = pltpu.make_async_copy(lift_hbm, lift, load_sem.at[2])
    ctr_copy = pltpu.make_async_copy(ctr_hbm, ctr, load_sem.at[3])
    clift_copy = pltpu.make_async_copy(clift_hbm, clift, load_sem.at[4])
    for copy in [kry_copy, lift_copy] + inv_copies + [otr_copy, ctr_copy, clift_copy]:
        copy.start()

    def current_rows(e):
        cur = kry[KB - 1, :, e, :]
        hi = cur.astype(jnp.bfloat16).astype(jnp.float32)
        return jnp.concatenate(
            [hi, cur - hi, jnp.zeros((8, B), jnp.float32)], axis=0
        ).astype(jnp.bfloat16)

    def offsets(trace, off):
        for e in range(E):
            off[e] = fold(dot_t(solved[e, 0, R : R + 2 * NV], trace[e]))

    def gains(trace, gain, off):
        for e in range(E):
            out = dot_t(solved[e, 0], trace[e]) + dot_t(solved[e, 1], trace[e])
            g_hi, g_lo = split(out[:R])
            gain[e, 0] = g_hi
            gain[e, 1] = g_lo
            off[e] = out[R : R + NV] + out[R + NV : R + 2 * NV]

    kry_copy.wait()
    lift_copy.wait()

    @pl.when(s == 0)
    def _():
        for e in range(E):
            if e % GROUP == 0:
                inv_copies[e // GROUP].wait()
            y = two_rows(fold(dot_t(current_rows(e), inv[e])[: 2 * NV]))
            solved[e, 0, R : R + 2 * NV] = y
        otr_copy.wait()
        offsets(otr, off_o)

    @pl.when(s > 0)
    def _():
        for e in range(E):
            if e % GROUP == 0:
                inv_copies[e // GROUP].wait()
            left = jnp.concatenate([lift[e], current_rows(e)], axis=0)
            hi, lo = split(dot_t(left, inv[e]))
            solved[e, 0] = hi
            solved[e, 1] = lo
        otr_copy.wait()

    @pl.when(lax.rem(s, S - 1) > 0)
    def _():
        gains(otr, gain_o, off_o)

    ctr_copy.wait()

    def gram():
        for n in range(NV):
            vs = [kry[k, n] for k in range(KB)]
            for i, (k, l) in enumerate(GRAM):
                row = NV * (KB + 1 + i) + n
                parts[row : row + 1, :] = lanes(vs[k] * vs[l])
        parts[NV * STATS :, :] = jnp.zeros((ROWS - NV * STATS, 128), jnp.float32)

    def lanes(x):
        x = jnp.sum(x, axis=0, keepdims=True)
        tail = jnp.concatenate([x[:, 256:B], jnp.zeros((1, 384 - B), jnp.float32)], axis=1)
        return x[:, :128] + x[:, 128:256] + tail

    @pl.when(lax.rem(s, S - 1) == 0)
    def _():
        pl.semaphore_wait(barrier, C * Q)

    @pl.when(lax.rem(s, S - 1) > 0)
    def _():
        pl.semaphore_wait(barrier, C * Q + 1)

    hop = pltpu.make_async_remote_copy(
        src_ref=outbuf,
        dst_ref=inbuf,
        send_sem=hop_sem.at[0],
        recv_sem=hop_sem.at[1],
        device_id=(lax.rem(s + 1, S), c, q),
        device_id_type=MESH,
    )

    def face_copy(dc, dq):
        span = pl.ds(place * E, E)
        return pltpu.make_async_remote_copy(
            src_ref=faces.at[span],
            dst_ref=faces.at[span],
            send_sem=face_sem.at[0],
            recv_sem=face_sem.at[1],
            device_id=(s, lax.rem(c + dc, C), lax.rem(q + dq, Q)),
            device_id_type=MESH,
        )

    def send_faces():
        for dc in range(C):
            for dq in range(Q):
                if dc or dq:
                    face_copy(dc, dq).start()

    @pl.when(s == 0)
    def _():
        for e in range(E):
            outbuf[e] = off_o[e]
        hop.start()
        offsets(ctr, off_c)
        for e in range(E):
            faces[place * E + e] = off_c[e]
        send_faces()
        gram()

    @pl.when(s > 0)
    def _():
        @pl.when(s > 1)
        def _():
            gains(ctr, gain_c, off_c)
            gram()

        hop.wait_recv()

        @pl.when(s < S - 1)
        def _():
            for e in range(E):
                x = two_rows(inbuf[up_ref[0, e]])
                outbuf[e] = off_o[e] - fold(dot(x, gain_o[e, 0]) + dot(x, gain_o[e, 1]))
            hop.start()

        @pl.when(s == 1)
        def _():
            gains(ctr, gain_c, off_c)

        for e in range(E):
            x = two_rows(inbuf[up_ref[0, e]])
            faces[place * E + e] = off_c[e] - fold(dot(x, gain_c[e, 0]) + dot(x, gain_c[e, 1]))
        send_faces()

        @pl.when(s == 1)
        def _():
            gram()

    @pl.when(s < S - 1)
    def _():
        pl.semaphore_wait(back_sem, 1)

    @pl.when(s > 0)
    def _():
        pl.semaphore_signal(back_sem, inc=1, device_id=(s - 1, c, q), device_id_type=MESH)

    clift_copy.wait()
    peers = C * Q - 1
    face_all = pltpu.make_async_remote_copy(
        src_ref=faces.at[pl.ds(0, peers * E)],
        dst_ref=faces.at[pl.ds(0, peers * E)],
        send_sem=face_sem.at[0],
        recv_sem=face_sem.at[1],
        device_id=(s, c, lax.rem(q + 1, Q)),
        device_id_type=MESH,
    )
    face_all.wait_recv()

    for e in range(E):
        x = two_rows(faces[cr_ref[0, e]])
        dbuf[:, e, :] = fold(dot(x, clift[e]))

    d_copy = pltpu.make_async_copy(dbuf, d_hbm, out_sem)
    d_copy.start()
    for n in range(NV):
        d = dbuf[n]
        for k in range(KB):
            parts[NV * k + n : NV * k + n + 1, :] = lanes(kry[k, n] * d)
        parts[NV * KB + n : NV * KB + n + 1, :] = lanes(d * d)

    diag = lax.broadcasted_iota(jnp.int32, (ROWS, 128), 0) == lax.broadcasted_iota(
        jnp.int32, (ROWS, 128), 1
    )
    column = jnp.sum(parts[...], axis=1, keepdims=True)
    stats[me] = jnp.sum(jnp.where(diag, column, 0.0), axis=0, keepdims=True)

    def stat_copy(peer):
        return pltpu.make_async_remote_copy(
            src_ref=stats.at[me],
            dst_ref=stats.at[me],
            send_sem=stat_sem.at[0],
            recv_sem=stat_sem.at[1],
            device_id=peer,
            device_id_type=MESH,
        )

    for peer in others():
        stat_copy(peer).start()
    stat_all = pltpu.make_async_remote_copy(
        src_ref=stats.at[pl.ds(0, total - 1)],
        dst_ref=stats.at[pl.ds(0, total - 1)],
        send_sem=stat_sem.at[0],
        recv_sem=stat_sem.at[1],
        device_id=(s, c, lax.rem(q + 1, Q)),
        device_id_type=MESH,
    )
    stat_all.wait_recv()

    row_ref[...] = jnp.sum(stats[...], axis=0)
    d_copy.wait()
    face_all.wait_send()
    stat_all.wait_send()

    @pl.when(s < S - 1)
    def _():
        hop.wait_send()


def finish(dofs, d_ref, row_ref, kry, next_ref, hess_ref):
    diag = lax.broadcasted_iota(jnp.int32, (ROWS, 128), 0) == lax.broadcasted_iota(
        jnp.int32, (ROWS, 128), 1
    )
    sums = jnp.sum(jnp.where(diag, row_ref[...], 0.0), axis=1, keepdims=True)
    at = lambda i: sums[NV * i : NV * (i + 1)]
    entry = {}
    for i, (k, l) in enumerate(GRAM):
        entry[k, l] = entry[l, k] = at(KB + 1 + i)
    coeffs = [(entry[k, KB - 1] + at(k)) / dofs for k in range(KB)]
    rest = [(1.0 if k == KB - 1 else 0.0) - coeffs[k] for k in range(KB)]
    squares = at(KB)
    for k in range(KB):
        inner = 2.0 * at(k)
        for l in range(KB):
            inner += rest[l] * entry[k, l]
        squares += rest[k] * inner
    norm = jnp.sqrt(jnp.maximum(squares, 0.0) / dofs + 1e-06)
    scale = 1.0 / norm
    weights = [r * scale for r in rest]
    for n in range(NV):
        out = d_ref[n] * scale[n : n + 1]
        for k in range(KB):
            out += kry[k, n] * weights[k][n : n + 1]
        next_ref[n] = out
    hess_ref[...] = jnp.concatenate(coeffs + [norm], axis=1)


def local(
    sizes,
    krylov_basis,
    inverse_blocks,
    inflow_lift,
    outflow_trace,
    cross_lift,
    cross_trace,
    upwind_element,
    cross_element,
):
    S, C, Q = sizes
    hbm = pl.BlockSpec(memory_space=pl.ANY)
    smem = pl.BlockSpec(memory_space=pltpu.SMEM)
    vmem = pl.BlockSpec(memory_space=pltpu.VMEM)
    bf16, f32 = jnp.bfloat16, jnp.float32
    basis = krylov_basis[:, :, 0]
    image, sums = pl.pallas_call(
        functools.partial(kernel, sizes),
        out_shape=(
            jax.ShapeDtypeStruct((NV, E, B), f32),
            jax.ShapeDtypeStruct((1, 128), f32),
        ),
        in_specs=[hbm] * 6 + [smem] * 2,
        out_specs=(hbm, vmem),
        scratch_shapes=[
            pltpu.VMEM((KB, NV, E, B), f32),
            pltpu.VMEM((E, B, B), bf16),
            pltpu.VMEM((E, R, B), bf16),
            pltpu.VMEM((E, R, B), bf16),
            pltpu.VMEM((E, R, B), bf16),
            pltpu.VMEM((E, R, B), bf16),
            pltpu.VMEM((E, 2, R + 16, B), bf16),
            pltpu.VMEM((E, 2, R, R), bf16),
            pltpu.VMEM((E, 2, R, R), bf16),
            pltpu.VMEM((E, NV, R), f32),
            pltpu.VMEM((E, NV, R), f32),
            pltpu.VMEM((E, NV, R), f32),
            pltpu.VMEM((E, NV, R), f32),
            pltpu.VMEM((C * Q * E, NV, R), f32),
            pltpu.VMEM((NV, E, B), f32),
            pltpu.VMEM((ROWS, 128), f32),
            pltpu.VMEM((S * C * Q, 1, 128), f32),
            pltpu.SemaphoreType.DMA((5 + E // GROUP,)),
            pltpu.SemaphoreType.DMA((2,)),
            pltpu.SemaphoreType.DMA((2,)),
            pltpu.SemaphoreType.DMA((2,)),
            pltpu.SemaphoreType.DMA,
            pltpu.SemaphoreType.REGULAR,
        ],
        compiler_params=pltpu.CompilerParams(collective_id=0, has_side_effects=True),
    )(
        basis,
        inverse_blocks[0],
        jnp.swapaxes(inflow_lift[0], 1, 2),
        outflow_trace[0],
        jnp.swapaxes(cross_lift[0], 1, 2),
        cross_trace[0],
        upwind_element,
        cross_element,
    )
    next_vector, hessenberg = pl.pallas_call(
        functools.partial(finish, float(E * B * S * C * Q)),
        out_shape=(
            jax.ShapeDtypeStruct((NV, E, B), f32),
            jax.ShapeDtypeStruct((NV, KB + 1), f32),
        ),
        in_specs=[vmem] * 3,
        out_specs=(vmem, vmem),
    )(image, sums, basis)
    return next_vector[:, None], hessenberg.T


def solution(mesh):
    sizes = tuple(mesh.shape[a] for a in ("stream", "cross", "pair"))
    return jax.shard_map(
        functools.partial(local, sizes),
        mesh=mesh,
        in_specs=(
            P(None, None, "stream", ("cross", "pair"), None),
            P("stream", ("cross", "pair"), None, None),
            P("stream", ("cross", "pair"), None, None),
            P("stream", ("cross", "pair"), None, None),
            P("stream", ("cross", "pair"), None, None),
            P("stream", ("cross", "pair"), None, None),
            P("stream", ("cross", "pair")),
            P("stream", ("cross", "pair")),
        ),
        out_specs=(P(None, "stream", ("cross", "pair"), None), P()),
        check_vma=False,
    )
```

```python
import functools

import jax
import jax.numpy as jnp
from jax import lax
from jax.experimental import pallas as pl
from jax.experimental.pallas import tpu as pltpu
from jax.sharding import PartitionSpec as P

E = 8
B = 320
R = 80
NV = 4
KB = 4
MESH = pl.DeviceIdType.MESH
GRAM = [(k, l) for k in range(KB) for l in range(k, KB)]
STATS = KB + 1 + len(GRAM)
ROWS = 64
GROUP = 2


def split(x):
    hi = x.astype(jnp.bfloat16)
    return hi, (x - hi.astype(jnp.float32)).astype(jnp.bfloat16)


def dot(a, b):
    return jnp.dot(a, b, preferred_element_type=jnp.float32)


def dot_t(a, b):
    return lax.dot_general(a, b, (((1,), (1,)), ((), ())), preferred_element_type=jnp.float32)


def two_rows(x):
    hi = x.astype(jnp.bfloat16).astype(jnp.float32)
    return jnp.concatenate([hi, x - hi], axis=0).astype(jnp.bfloat16)


def fold(x):
    return x[:NV] + x[NV:]


def kernel(
    sizes,
    kry_hbm,
    inv_hbm,
    lift_hbm,
    otr_hbm,
    clift_hbm,
    ctr_hbm,
    up_ref,
    cr_ref,
    d_hbm,
    row_ref,
    kry,
    inv,
    lift,
    otr,
    clift,
    ctr,
    solved,
    gain_o,
    gain_c,
    off_o,
    off_c,
    outbuf,
    inbuf,
    faces,
    dbuf,
    parts,
    stats,
    load_sem,
    hop_sem,
    face_sem,
    stat_sem,
    out_sem,
    back_sem,
):
    S, C, Q = sizes
    total = S * C * Q
    s = lax.axis_index("stream")
    c = lax.axis_index("cross")
    q = lax.axis_index("pair")
    place = c * Q + q
    me = s * (C * Q) + place

    barrier = pltpu.get_barrier_semaphore()

    def others():
        for ds in [*range(1, S), 0]:
            for dc in [*range(1, C), 0]:
                for dq in [*range(1, Q), 0]:
                    if ds or dc or dq:
                        yield (lax.rem(s + ds, S), lax.rem(c + dc, C), lax.rem(q + dq, Q))

    for dc in range(C):
        for dq in range(Q):
            if dc or dq:
                pl.semaphore_signal(
                    barrier,
                    inc=1,
                    device_id=(s, lax.rem(c + dc, C), lax.rem(q + dq, Q)),
                    device_id_type=MESH,
                )
    for edge, step in ((S - 1, 1), (0, S - 1)):

        @pl.when(s != edge)
        def _():
            pl.semaphore_signal(
                barrier, inc=1, device_id=(lax.rem(s + step, S), c, q), device_id_type=MESH
            )

    last, rest = pl.ds(KB - 1, 1), pl.ds(0, KB - 1)
    current_copy = pltpu.make_async_copy(kry_hbm.at[last], kry.at[last], load_sem.at[0])
    kry_copy = pltpu.make_async_copy(kry_hbm.at[rest], kry.at[rest], load_sem.at[5 + E // GROUP])
    inv_copies = [
        pltpu.make_async_copy(
            inv_hbm.at[pl.ds(g * GROUP, GROUP)], inv.at[pl.ds(g * GROUP, GROUP)], load_sem.at[5 + g]
        )
        for g in range(E // GROUP)
    ]
    otr_copy = pltpu.make_async_copy(otr_hbm, otr, load_sem.at[1])
    lift_copy = pltpu.make_async_copy(lift_hbm, lift, load_sem.at[2])
    ctr_copy = pltpu.make_async_copy(ctr_hbm, ctr, load_sem.at[3])
    clift_copy = pltpu.make_async_copy(clift_hbm, clift, load_sem.at[4])
    current_copy.start()

    @pl.when(s == 0)
    def _():
        for copy in inv_copies + [otr_copy, ctr_copy, lift_copy]:
            copy.start()

    @pl.when(s > 0)
    def _():
        for copy in [lift_copy] + inv_copies + [otr_copy, ctr_copy]:
            copy.start()

    kry_copy.start()
    clift_copy.start()

    def current_rows(e):
        cur = kry[KB - 1, :, e, :]
        hi = cur.astype(jnp.bfloat16).astype(jnp.float32)
        return jnp.concatenate(
            [hi, cur - hi, jnp.zeros((8, B), jnp.float32)], axis=0
        ).astype(jnp.bfloat16)

    def offsets(trace, off):
        for e in range(E):
            off[e] = fold(dot_t(solved[e, 0, R : R + 2 * NV], trace[e]))

    def gains(trace, gain, off):
        for e in range(E):
            out = dot_t(solved[e, 0], trace[e]) + dot_t(solved[e, 1], trace[e])
            g_hi, g_lo = split(out[:R])
            gain[e, 0] = g_hi
            gain[e, 1] = g_lo
            off[e] = out[R : R + NV] + out[R + NV : R + 2 * NV]

    current_copy.wait()

    @pl.when(s == 0)
    def _():
        for e in range(E):
            if e % GROUP == 0:
                inv_copies[e // GROUP].wait()
            y = two_rows(fold(dot_t(current_rows(e), inv[e])[: 2 * NV]))
            solved[e, 0, R : R + 2 * NV] = y
        otr_copy.wait()
        offsets(otr, off_o)

    @pl.when(s > 0)
    def _():
        lift_copy.wait()
        for e in range(E):
            if e % GROUP == 0:
                inv_copies[e // GROUP].wait()
            left = jnp.concatenate([lift[e], current_rows(e)], axis=0)
            hi, lo = split(dot_t(left, inv[e]))
            solved[e, 0] = hi
            solved[e, 1] = lo
        otr_copy.wait()

    @pl.when(lax.rem(s, S - 1) > 0)
    def _():
        gains(otr, gain_o, off_o)

    def gram():
        for n in range(NV):
            vs = [kry[k, n] for k in range(KB)]
            for i, (k, l) in enumerate(GRAM):
                row = NV * (KB + 1 + i) + n
                parts[row : row + 1, :] = lanes(vs[k] * vs[l])
        parts[NV * STATS :, :] = jnp.zeros((ROWS - NV * STATS, 128), jnp.float32)

    def lanes(x):
        x = jnp.sum(x, axis=0, keepdims=True)
        tail = jnp.concatenate([x[:, 256:B], jnp.zeros((1, 384 - B), jnp.float32)], axis=1)
        return x[:, :128] + x[:, 128:256] + tail

    @pl.when(lax.rem(s, S - 1) == 0)
    def _():
        pl.semaphore_wait(barrier, C * Q)

    @pl.when(lax.rem(s, S - 1) > 0)
    def _():
        pl.semaphore_wait(barrier, C * Q + 1)

    hop = pltpu.make_async_remote_copy(
        src_ref=outbuf,
        dst_ref=inbuf,
        send_sem=hop_sem.at[0],
        recv_sem=hop_sem.at[1],
        device_id=(lax.rem(s + 1, S), c, q),
        device_id_type=MESH,
    )

    def face_copy(dc, dq):
        span = pl.ds(place * E, E)
        return pltpu.make_async_remote_copy(
            src_ref=faces.at[span],
            dst_ref=faces.at[span],
            send_sem=face_sem.at[0],
            recv_sem=face_sem.at[1],
            device_id=(s, lax.rem(c + dc, C), lax.rem(q + dq, Q)),
            device_id_type=MESH,
        )

    def send_faces():
        for dc in range(C):
            for dq in range(Q):
                if dc or dq:
                    face_copy(dc, dq).start()

    @pl.when(s == 0)
    def _():
        for e in range(E):
            outbuf[e] = off_o[e]
        hop.start()
        ctr_copy.wait()
        offsets(ctr, off_c)
        for e in range(E):
            faces[place * E + e] = off_c[e]
        send_faces()
        lift_copy.wait()
        kry_copy.wait()
        gram()

    @pl.when(s > 0)
    def _():
        ctr_copy.wait()
        kry_copy.wait()

        @pl.when(s > 1)
        def _():
            gains(ctr, gain_c, off_c)
            gram()

        hop.wait_recv()

        @pl.when(s < S - 1)
        def _():
            for e in range(E):
                x = two_rows(inbuf[up_ref[0, e]])
                outbuf[e] = off_o[e] - fold(dot(x, gain_o[e, 0]) + dot(x, gain_o[e, 1]))
            hop.start()

        @pl.when(s == 1)
        def _():
            gains(ctr, gain_c, off_c)

        for e in range(E):
            x = two_rows(inbuf[up_ref[0, e]])
            faces[place * E + e] = off_c[e] - fold(dot(x, gain_c[e, 0]) + dot(x, gain_c[e, 1]))
        send_faces()

        @pl.when(s == 1)
        def _():
            gram()

    @pl.when(s < S - 1)
    def _():
        pl.semaphore_wait(back_sem, 1)

    @pl.when(s > 0)
    def _():
        pl.semaphore_signal(back_sem, inc=1, device_id=(s - 1, c, q), device_id_type=MESH)

    clift_copy.wait()
    peers = C * Q - 1
    face_all = pltpu.make_async_remote_copy(
        src_ref=faces.at[pl.ds(0, peers * E)],
        dst_ref=faces.at[pl.ds(0, peers * E)],
        send_sem=face_sem.at[0],
        recv_sem=face_sem.at[1],
        device_id=(s, c, lax.rem(q + 1, Q)),
        device_id_type=MESH,
    )
    face_all.wait_recv()

    for e in range(E):
        x = two_rows(faces[cr_ref[0, e]])
        dbuf[:, e, :] = fold(dot(x, clift[e]))

    d_copy = pltpu.make_async_copy(dbuf, d_hbm, out_sem)
    d_copy.start()
    for n in range(NV):
        d = dbuf[n]
        for k in range(KB):
            parts[NV * k + n : NV * k + n + 1, :] = lanes(kry[k, n] * d)
        parts[NV * KB + n : NV * KB + n + 1, :] = lanes(d * d)

    diag = lax.broadcasted_iota(jnp.int32, (ROWS, 128), 0) == lax.broadcasted_iota(
        jnp.int32, (ROWS, 128), 1
    )
    column = jnp.sum(parts[...], axis=1, keepdims=True)
    stats[me] = jnp.sum(jnp.where(diag, column, 0.0), axis=0, keepdims=True)

    def stat_copy(peer):
        return pltpu.make_async_remote_copy(
            src_ref=stats.at[me],
            dst_ref=stats.at[me],
            send_sem=stat_sem.at[0],
            recv_sem=stat_sem.at[1],
            device_id=peer,
            device_id_type=MESH,
        )

    for peer in others():
        stat_copy(peer).start()
    stat_all = pltpu.make_async_remote_copy(
        src_ref=stats.at[pl.ds(0, total - 1)],
        dst_ref=stats.at[pl.ds(0, total - 1)],
        send_sem=stat_sem.at[0],
        recv_sem=stat_sem.at[1],
        device_id=(s, c, lax.rem(q + 1, Q)),
        device_id_type=MESH,
    )
    stat_all.wait_recv()

    row_ref[...] = jnp.sum(stats[...], axis=0)
    d_copy.wait()
    face_all.wait_send()
    stat_all.wait_send()

    @pl.when(s < S - 1)
    def _():
        hop.wait_send()


def finish(dofs, d_ref, row_ref, kry, next_ref, hess_ref):
    diag = lax.broadcasted_iota(jnp.int32, (ROWS, 128), 0) == lax.broadcasted_iota(
        jnp.int32, (ROWS, 128), 1
    )
    sums = jnp.sum(jnp.where(diag, row_ref[...], 0.0), axis=1, keepdims=True)
    at = lambda i: sums[NV * i : NV * (i + 1)]
    entry = {}
    for i, (k, l) in enumerate(GRAM):
        entry[k, l] = entry[l, k] = at(KB + 1 + i)
    coeffs = [(entry[k, KB - 1] + at(k)) / dofs for k in range(KB)]
    rest = [(1.0 if k == KB - 1 else 0.0) - coeffs[k] for k in range(KB)]
    squares = at(KB)
    for k in range(KB):
        inner = 2.0 * at(k)
        for l in range(KB):
            inner += rest[l] * entry[k, l]
        squares += rest[k] * inner
    norm = jnp.sqrt(jnp.maximum(squares, 0.0) / dofs + 1e-06)
    scale = 1.0 / norm
    weights = [r * scale for r in rest]
    for n in range(NV):
        out = d_ref[n] * scale[n : n + 1]
        for k in range(KB):
            out += kry[k, n] * weights[k][n : n + 1]
        next_ref[n] = out
    hess_ref[...] = jnp.concatenate(coeffs + [norm], axis=1)


def local(
    sizes,
    krylov_basis,
    inverse_blocks,
    inflow_lift,
    outflow_trace,
    cross_lift,
    cross_trace,
    upwind_element,
    cross_element,
):
    S, C, Q = sizes
    hbm = pl.BlockSpec(memory_space=pl.ANY)
    smem = pl.BlockSpec(memory_space=pltpu.SMEM)
    vmem = pl.BlockSpec(memory_space=pltpu.VMEM)
    bf16, f32 = jnp.bfloat16, jnp.float32
    basis = krylov_basis[:, :, 0]
    image, sums = pl.pallas_call(
        functools.partial(kernel, sizes),
        out_shape=(
            jax.ShapeDtypeStruct((NV, E, B), f32),
            jax.ShapeDtypeStruct((1, 128), f32),
        ),
        in_specs=[hbm] * 6 + [smem] * 2,
        out_specs=(hbm, vmem),
        scratch_shapes=[
            pltpu.VMEM((KB, NV, E, B), f32),
            pltpu.VMEM((E, B, B), bf16),
            pltpu.VMEM((E, R, B), bf16),
            pltpu.VMEM((E, R, B), bf16),
            pltpu.VMEM((E, R, B), bf16),
            pltpu.VMEM((E, R, B), bf16),
            pltpu.VMEM((E, 2, R + 16, B), bf16),
            pltpu.VMEM((E, 2, R, R), bf16),
            pltpu.VMEM((E, 2, R, R), bf16),
            pltpu.VMEM((E, NV, R), f32),
            pltpu.VMEM((E, NV, R), f32),
            pltpu.VMEM((E, NV, R), f32),
            pltpu.VMEM((E, NV, R), f32),
            pltpu.VMEM((C * Q * E, NV, R), f32),
            pltpu.VMEM((NV, E, B), f32),
            pltpu.VMEM((ROWS, 128), f32),
            pltpu.VMEM((S * C * Q, 1, 128), f32),
            pltpu.SemaphoreType.DMA((6 + E // GROUP,)),
            pltpu.SemaphoreType.DMA((2,)),
            pltpu.SemaphoreType.DMA((2,)),
            pltpu.SemaphoreType.DMA((2,)),
            pltpu.SemaphoreType.DMA,
            pltpu.SemaphoreType.REGULAR,
        ],
        compiler_params=pltpu.CompilerParams(collective_id=0, has_side_effects=True),
    )(
        basis,
        inverse_blocks[0],
        jnp.swapaxes(inflow_lift[0], 1, 2),
        outflow_trace[0],
        jnp.swapaxes(cross_lift[0], 1, 2),
        cross_trace[0],
        upwind_element,
        cross_element,
    )
    next_vector, hessenberg = pl.pallas_call(
        functools.partial(finish, float(E * B * S * C * Q)),
        out_shape=(
            jax.ShapeDtypeStruct((NV, E, B), f32),
            jax.ShapeDtypeStruct((NV, KB + 1), f32),
        ),
        in_specs=[vmem] * 3,
        out_specs=(vmem, vmem),
    )(image, sums, basis)
    return next_vector[:, None], hessenberg.T


def solution(mesh):
    sizes = tuple(mesh.shape[a] for a in ("stream", "cross", "pair"))
    return jax.shard_map(
        functools.partial(local, sizes),
        mesh=mesh,
        in_specs=(
            P(None, None, "stream", ("cross", "pair"), None),
            P("stream", ("cross", "pair"), None, None),
            P("stream", ("cross", "pair"), None, None),
            P("stream", ("cross", "pair"), None, None),
            P("stream", ("cross", "pair"), None, None),
            P("stream", ("cross", "pair"), None, None),
            P("stream", ("cross", "pair")),
            P("stream", ("cross", "pair")),
        ),
        out_specs=(P(None, "stream", ("cross", "pair"), None), P()),
        check_vma=False,
    )
```
